128 devices in a mesh: wide: 8 (over z, core), narrow: 16 (over y, x).
Axes of the slice: x: 4, y: 4, z: 4, core: 2. Of those that a mesh axis runs over, the one named last changes fastest.
Arguments:
- sources: bfloat16 [131072, 768], P(('wide', 'narrow')), as said below
- targets: bfloat16 [131072, 768], P(('wide', 'narrow')), as said below
- target_lists: int32 [1024, 4], P(('wide', 'narrow')), may hold values from 0 to 1023, as said below
- target_clusters: int32 [131072], P(('wide', 'narrow')), may hold values from 0 to 8191
- centroids_src: bfloat16 [8192, 768], P(('wide', 'narrow')), may hold values from -6 to 6
- centroids_tgt: bfloat16 [8192, 768], P('narrow', 'wide'), may hold values from -6 to 6
- sender_mean_measure: float32 [8192], P('wide'), may hold values from 0.05 to 20
- recipient_mean_measure: float32 [8192], P('narrow'), may hold values from 0.05 to 20
Outputs:
- src_bary: bfloat16 [131072, 768], P(('wide', 'narrow'))
- tgt_bary: bfloat16 [131072, 768], P(('wide', 'narrow'))
- src_potential: float32 [131072], P(('wide', 'narrow'))
- tgt_potential: float32 [131072], P(('wide', 'narrow'))
The draws below stay inside these ranges and needn't reach their ends.
Inputs may be any that keep to these rules, and one draw needn't show every extreme that they name: `target_lists`: target block t holds targets t * 128 to (t + 1) * 128 - 1. Every entry names a block held by a device with the same wide index as the device of the source block. Among the 32 entries of one device, at most 3 name blocks held by any one device, and on every device some device is named by exactly 3. Every target block is named by at least one entry. `sources`: Real-valued features. `targets`: Real-valued features.
All inputs are finite; a program needn't handle non-finite values.
Results may differ from the reference program's by a relative error of at most 0.007.
Values may be sent and summed in bfloat16 or wider, within the bound.
No kernel may reach another device: no remote copies, remote signals or barrier semaphores. Data moves between devices by JAX's collectives and lax.ppermute only.
A program may use at most 128 MiB of HBM per device.

```python
import math
import jax
import jax.numpy as jnp
from jax import lax

D = 768
KC = 8192
BLK = 128
LIST = 4
ITC = 6
STEPS = 3
NB_DEV = 8
TB_DEV = 8
CAP = 3
NBLK = 1024
NS = 131072
NT = 131072
N_NARROW = 16


def feature_rows(key, row_count):
    values = jax.random.normal(key, (row_count, D), jnp.float32)
    return values.astype(jnp.bfloat16)


def draw_sources(key, part):
    return feature_rows(jax.random.fold_in(key, 101), NS)


def draw_targets(key, part):
    return feature_rows(jax.random.fold_in(key, 202), NT)


def draw_target_lists(key, part):
    device_count = NBLK // NB_DEV
    pool_size = N_NARROW * CAP
    entry_count = NB_DEV * LIST
    shifts = jax.random.randint(jax.random.fold_in(key, 7), (device_count // N_NARROW,), 0, N_NARROW)

    def one_device(device):
        device_key = jax.random.fold_in(key, device + 11)
        first_key, second_key, third_key = jax.random.split(device_key, 3)
        wide_index = device // N_NARROW
        narrow_index = device % N_NARROW
        pool_index = jnp.arange(pool_size)
        owner_of = pool_index // CAP
        copy_of = pool_index % CAP
        relative = (owner_of - narrow_index - shifts[wide_index]) % N_NARROW
        block_cover = relative + N_NARROW * copy_of
        covering = block_cover < TB_DEV
        forced = jnp.logical_or(covering, relative == 0)
        order_key = jax.random.permutation(first_key, pool_size)
        rank_of = jnp.zeros((pool_size,), jnp.int32).at[order_key].set(pool_index.astype(jnp.int32))
        score = jnp.where(forced, 0, 1) * pool_size + rank_of
        chosen = jnp.argsort(score)[:entry_count]
        random_local = jax.random.randint(second_key, (pool_size,), 0, TB_DEV)
        local_block = jnp.where(covering, block_cover, random_local)
        block_ids = (wide_index * N_NARROW + owner_of) * TB_DEV + local_block
        picked = block_ids[chosen]
        placed = picked[jax.random.permutation(third_key, entry_count)]
        return placed.reshape(NB_DEV, LIST)
    return jax.vmap(one_device)(jnp.arange(device_count)).reshape(NBLK, LIST).astype(jnp.int32)


def place_ends(array, own_key, smallest, largest):
    extent = array.shape
    spot = [jax.random.randint(jax.random.fold_in(own_key, axis), (), 0, extent[axis]) for axis in range(len(extent))]
    array = array.at[tuple(spot)].set(smallest)
    longest = extent.index(max(extent))
    spot[longest] = (spot[longest] + 1) % extent[longest]
    return array.at[tuple(spot)].set(largest)


def levels(own_key, shape, cuts, least, high):
    factor_of, own = 1.0, jax.random.fold_in(own_key, 6)
    for axis_at, blocks in cuts:
        heights = jnp.exp(jax.random.uniform(jax.random.fold_in(own, axis_at), (blocks,), jnp.float32, least / len(cuts), high / len(cuts)))
        factor_of = factor_of * jnp.repeat(heights, shape[axis_at] // blocks).reshape([-1 if axis == axis_at else 1 for axis in range(len(shape))])
    return factor_of


def centred(own_key, extent, spread, limit, pieces=(), dtype=jnp.bfloat16):
    level = levels(own_key, extent, pieces, -0.22, 0.18) if pieces else 1.0
    drawn = jax.random.normal(own_key, extent, jnp.float32) * spread * level
    return jnp.minimum(jnp.maximum(drawn, -limit), limit).astype(dtype)


def setup_inputs(seed: int = 0) -> dict:
    seeds = jax.random.split(jax.random.key(seed), 9)
    return {
        "sources": draw_sources(jax.random.fold_in(seeds[8], 71), 0),
        "targets": draw_targets(jax.random.fold_in(seeds[8], 71), 0),
        "target_lists": draw_target_lists(jax.random.fold_in(seeds[8], 71), 0),
        "target_clusters": place_ends(jax.random.randint(seeds[3], (NT,), 0, KC), jax.random.fold_in(seeds[3], 1), 0, KC - 1).astype(jnp.int32),
        "centroids_src": centred(seeds[4], (KC, D), 1.0, 6.0, ((0, 128),)),
        "centroids_tgt": centred(seeds[5], (KC, D), 1.0, 6.0, ((0, 16), (1, 8))),
        "sender_mean_measure": jnp.clip(jnp.exp(math.log(20.0) - 5.9914645 * jax.random.uniform(seeds[6], (KC,), jnp.float32) ** levels(seeds[6], (KC,), ((0, 8),), -0.2, 0.2)), 0.05, 20.0),
        "recipient_mean_measure": jnp.clip(jnp.exp(math.log(20.0) - 5.9914645 * jax.random.uniform(seeds[7], (KC,), jnp.float32) ** levels(seeds[7], (KC,), ((0, 16),), -0.2, 0.2)), 0.05, 20.0),
    }


heat_parameter = 0.02


def pair_cost(left_rows, right_rows):
    feature_count = left_rows.shape[1]
    left_sq = jnp.sum(jnp.square(left_rows.astype(jnp.float32)), axis=1)
    right_sq = jnp.sum(jnp.square(right_rows.astype(jnp.float32)), axis=1)
    cross_term = jnp.dot(left_rows, right_rows.T, preferred_element_type=jnp.float32)
    return (left_sq[:, None] + right_sq[None, :] - 2.0 * cross_term) / feature_count


def reference(sources, targets, target_lists, target_clusters, centroids_src, centroids_tgt, sender_mean_measure, recipient_mean_measure):
    feature_count = sources.shape[1]
    blurred_stratum = pair_cost(centroids_src, centroids_tgt)
    ln_sender_measure = heat_parameter * jnp.log(sender_mean_measure)
    ln_recipient_measure = heat_parameter * jnp.log(recipient_mean_measure)

    def coarse_turn(iteration, recipient_blurred_stratum):
        sender_blurred_stratum = ln_sender_measure - heat_parameter * jax.nn.logsumexp((recipient_blurred_stratum[None, :] - blurred_stratum) / heat_parameter, axis=1)
        return ln_recipient_measure - heat_parameter * jax.nn.logsumexp((sender_blurred_stratum[:, None] - blurred_stratum) / heat_parameter, axis=0)

    coarse_pot = lax.fori_loop(0, ITC, coarse_turn, jnp.zeros((KC,), jnp.float32))
    src_blocks = sources.reshape(NBLK, BLK, feature_count)
    tgt_blocks = targets.reshape(NBLK, BLK, feature_count)
    flat_lists = target_lists.reshape(-1)

    def entry_cost(block_pair):
        block_rows, block_list = block_pair
        listed = tgt_blocks[block_list]
        left_sq = jnp.sum(jnp.square(block_rows.astype(jnp.float32)), axis=1)
        right_sq = jnp.sum(jnp.square(listed.astype(jnp.float32)), axis=2)
        cross_term = jnp.einsum("id,lcd->lic", block_rows.astype(jnp.float32), listed.astype(jnp.float32))
        return (left_sq[None, :, None] + right_sq[:, None, :] - 2.0 * cross_term) / feature_count

    pointwise_charge = lax.map(entry_cost, (src_blocks, target_lists))
    recipient_kantorovich = coarse_pot[target_clusters].reshape(NBLK, BLK)

    def half_turn(block_pair):
        bandwise_charge, named_kantorovich = block_pair
        sender_figures = -heat_parameter * jax.nn.logsumexp((named_kantorovich[:, None, :] - bandwise_charge) / heat_parameter, axis=(0, 2))
        segment_lse_fold = jax.nn.logsumexp((sender_figures[None, :, None] - bandwise_charge) / heat_parameter, axis=1)
        return sender_figures, segment_lse_fold

    sender_kantorovich = jnp.zeros((NBLK, BLK), jnp.float32)
    for iteration in range(STEPS):
        sender_kantorovich, segment_lse_fold = lax.map(half_turn, (pointwise_charge, recipient_kantorovich[target_lists]))
        flat_part = segment_lse_fold.reshape(-1, BLK)
        best_rating = jnp.full((NBLK, BLK), -jnp.inf, jnp.float32).at[flat_lists].max(flat_part)
        ongoing_additions = jnp.zeros((NBLK, BLK), jnp.float32).at[flat_lists].add(jnp.exp(flat_part - best_rating[flat_lists]))
        recipient_kantorovich = -heat_parameter * (best_rating + jnp.log(ongoing_additions))
    listed_final = recipient_kantorovich[target_lists]

    def bary_turn(carry, block_items):
        numerators, denominators = carry
        block_rows, block_list, bandwise_charge, sender_band_members, named_kantorovich = block_items
        joint_measure_shares_entrywise = jnp.exp((sender_band_members[None, :, None] + named_kantorovich[:, None, :] - bandwise_charge) / heat_parameter).astype(jnp.bfloat16)
        weights_wide = lax.optimization_barrier(joint_measure_shares_entrywise).astype(jnp.float32)
        listed = tgt_blocks[block_list].astype(jnp.float32)
        src_num = jnp.einsum("lic,lcd->id", weights_wide, listed)
        src_den = jnp.sum(weights_wide, axis=(0, 2))
        src_mean = (src_num / src_den[:, None]).astype(jnp.bfloat16)
        tgt_part = jnp.einsum("lic,id->lcd", weights_wide, block_rows.astype(jnp.float32)).astype(jnp.bfloat16)
        tgt_part = lax.optimization_barrier(tgt_part).astype(jnp.float32)
        tgt_weight = jnp.sum(weights_wide, axis=1).astype(jnp.bfloat16)
        tgt_weight = lax.optimization_barrier(tgt_weight).astype(jnp.float32)
        return (numerators.at[block_list].add(tgt_part), denominators.at[block_list].add(tgt_weight)), src_mean

    initial = (jnp.zeros((NBLK, BLK, feature_count), jnp.float32), jnp.zeros((NBLK, BLK), jnp.float32))
    (numerators, denominators), src_means = lax.scan(bary_turn, initial, (src_blocks, target_lists, pointwise_charge, sender_kantorovich, listed_final))
    src_bary = src_means.reshape(NS, feature_count)
    tgt_bary = (numerators / denominators[:, :, None]).astype(jnp.bfloat16).reshape(NT, feature_count)
    return src_bary, tgt_bary, sender_kantorovich.reshape(NS), recipient_kantorovich.reshape(NT)
```

```python
import functools

import jax
import jax.numpy as jnp
from jax import lax
from jax.experimental import pallas as pl
from jax.experimental.pallas import tpu as pltpu
from jax.sharding import Mesh
from jax.sharding import PartitionSpec as P

BLK = 128
LIST = 4
ITC = 6
STEPS = 3
CAP = 3
HEAT = 0.02
SIDE = 4
OWN = 8
GROUP = SIDE * OWN
UNROLL = 4
SLOTS = SIDE * SIDE * CAP + UNROLL
HALF = OWN // 2
HALF_ROWS = HALF * BLK + 16
FAR = (4, 5)
NEAR = (2, 7, 3, 6, 0, 1)
NEG = -1e30
AT_SRC, AT_TGT, AT_START, AT_COUNT, AT_LIST, AT_LIVE, TABLE = 0, 64, 128, 168, 200, 712, 768
LINES = 3 * OWN + 1

F32 = jnp.float32
BF16 = jnp.bfloat16


def spec(n):
    return [pl.BlockSpec(memory_space=pltpu.VMEM)] * n


def smem(n):
    return [pl.BlockSpec(memory_space=pltpu.SMEM)] * n


def columns_of(rows):
    count = rows.shape[0]
    if count < BLK:
        rows = jnp.concatenate([rows, jnp.zeros((BLK - count, BLK), F32)], axis=0)
    return rows.T


def spread(col_ref, columns, count):
    for k in range(count):
        col_ref[k] = jnp.broadcast_to(columns[:, k : k + 1], (BLK, BLK))


def joined(parts_ref):
    count = parts_ref.shape[0]
    top = parts_ref[0]
    for k in range(1, count):
        top = jnp.maximum(top, parts_ref[k])
    total = jnp.exp(parts_ref[0] - top)
    for k in range(1, count):
        total = total + jnp.exp(parts_ref[k] - top)
    return top + jnp.log(total)


def tree(parts, op):
    while len(parts) > 1:
        parts = [op(a, b) for a, b in zip(parts[::2], parts[1::2])] + (
            [parts[-1]] if len(parts) % 2 else []
        )
    return parts[0]


def coarse_cost_kernel(scale, place_ref, x_ref, *refs):
    pieces, (by_col_ref, by_row_ref, y_ref, ysq_ref) = refs[:SIDE], refs[SIDE:]
    z, core = place_ref[2], place_ref[3]
    depth, cols = pieces[0].shape[1], y_ref.shape[1] // BLK
    for away in range(SIDE):
        home = lax.rem(z + SIDE - away, SIDE) * 2
        for twin in range(2):
            at = (home + lax.rem(core + twin, 2)) * depth
            y_ref[pl.ds(pl.multiple_of(at, depth), depth), :] = pieces[away][twin]
    for k in range(cols):
        wide_y = y_ref[:, k * BLK : (k + 1) * BLK].astype(F32)
        ysq_ref[k : k + 1, :] = jnp.sum(wide_y * wide_y, axis=0, keepdims=True)
    tall = 2 * BLK

    def one(j, carry):
        x = x_ref[pl.ds(pl.multiple_of(j * tall, tall), tall), :]
        wide_x = x.astype(F32)
        x_sq = jnp.sum(wide_x * wide_x, axis=1, keepdims=True)
        for k in range(cols):
            y = y_ref[:, k * BLK : (k + 1) * BLK]
            cross = jnp.dot(x, y, preferred_element_type=F32)
            cost = (x_sq + ysq_ref[k : k + 1, :] - 2.0 * cross) * scale
            by_col_ref[k, pl.ds(pl.multiple_of(j * tall, tall), tall), :] = cost
            for h in range(2):
                by_row_ref[2 * j + h, k * BLK : (k + 1) * BLK, :] = cost[
                    h * BLK : (h + 1) * BLK, :
                ].T
        return carry

    lax.fori_loop(0, x_ref.shape[0] // tall, one, 0)


def coarse_costs(place, x, pieces, scale):
    rows, cols = x.shape[0] // BLK, pieces[0].shape[2] // BLK
    return pl.pallas_call(
        functools.partial(coarse_cost_kernel, scale),
        out_shape=(
            jax.ShapeDtypeStruct((cols, rows * BLK, BLK), F32),
            jax.ShapeDtypeStruct((rows, cols * BLK, BLK), F32),
        ),
        in_specs=smem(1) + spec(1 + SIDE),
        out_specs=tuple(spec(2)),
        scratch_shapes=[
            pltpu.VMEM((x.shape[1], cols * BLK), BF16),
            pltpu.VMEM((8, BLK), F32),
        ],
        compiler_params=pltpu.CompilerParams(vmem_limit_bytes=20 << 20),
        name="coarse_costs",
    )(place, x, *pieces)


def coarse_half_kernel(first, recv_ref, mass_ref, cost_ref, out_ref, col_ref, res_ref):
    given = mass_ref.shape[0]
    chunks = cost_ref.shape[0]
    if first:
        potential = jnp.zeros((given, BLK), F32)
    else:
        potential = jnp.log(mass_ref[...]) - joined(recv_ref)
    spread(col_ref, columns_of(potential), given)

    def chunk(c, carry):
        def piece(k):
            cost = cost_ref[c, k * BLK : (k + 1) * BLK, :]
            return (col_ref[k] - cost).reshape(BLK // 8, 8, BLK)

        top = tree([jnp.max(piece(k), axis=0) for k in range(given)], jnp.maximum)
        total = tree(
            [jnp.sum(jnp.exp(piece(k) - top[None]), axis=0) for k in range(given)], jnp.add
        )
        best = jnp.max(top, axis=0, keepdims=True)
        total = jnp.sum(total * jnp.exp(top - best), axis=0, keepdims=True)
        res_ref[pl.ds(c, 1), :] = best + jnp.log(total)
        return carry

    lax.fori_loop(0, chunks, chunk, 0)
    result = res_ref[0:chunks, :]
    for k in range(out_ref.shape[0]):
        out_ref[k] = result


def coarse_half(first, recv, mass, cost, copies):
    given, chunks = mass.shape[0], cost.shape[0]
    return pl.pallas_call(
        functools.partial(coarse_half_kernel, first),
        out_shape=jax.ShapeDtypeStruct((copies, chunks, BLK), F32),
        in_specs=spec(3),
        out_specs=spec(1)[0],
        scratch_shapes=[pltpu.VMEM((given, BLK, BLK), F32), pltpu.VMEM((8, BLK), F32)],
        compiler_params=pltpu.CompilerParams(vmem_limit_bytes=12 << 20),
        name="coarse_half",
    )(recv, mass, cost)


def coarse_end_kernel(recv_ref, mass_ref, out_ref):
    potential = jnp.log(mass_ref[...]) - joined(recv_ref)
    for k in range(out_ref.shape[0]):
        out_ref[k] = potential


def coarse_end(recv, mass, copies):
    return pl.pallas_call(
        coarse_end_kernel,
        out_shape=jax.ShapeDtypeStruct((copies, *mass.shape), F32),
        in_specs=spec(2),
        out_specs=spec(1)[0],
        name="coarse_end",
    )(recv, mass)


def plan_kernel(lists_ref, place_ref, table_ref):
    y = place_ref[0]

    def clear(k, carry):
        for j in range(8):
            table_ref[k * 8 + j] = 0
        return carry

    lax.fori_loop(0, TABLE // 8, clear, 0)

    def scan(q, live):
        block = lists_ref[q]
        device = lax.rem(lax.div(block, OWN), SIDE * SIDE)
        here = (lax.div(device, SIDE) == y).astype(jnp.int32)
        s = lax.div(q, LIST)
        t = lax.rem(device, SIDE) * OWN + lax.rem(block, OWN)
        table_ref[AT_SRC + live] = s
        table_ref[AT_TGT + live] = t
        seen = table_ref[AT_COUNT + t]
        table_ref[AT_LIST + t * 16 + seen] = live
        table_ref[AT_COUNT + t] = seen + here
        live = live + here
        table_ref[AT_START + s + 1] = live
        return live

    live = lax.fori_loop(0, SIDE * OWN * LIST, scan, 0)
    for k in range(UNROLL + 1):
        table_ref[AT_SRC + live + k] = GROUP
        table_ref[AT_TGT + live + k] = GROUP
    table_ref[AT_LIVE] = live


def entry_table(lists, place):
    return pl.pallas_call(
        plan_kernel,
        out_shape=jax.ShapeDtypeStruct((TABLE,), jnp.int32),
        in_specs=smem(2),
        out_specs=smem(1)[0],
        name="entry_table",
    )(lists, place)


def fine_cost_kernel(scale, table_ref, x_ref, y_ref, xsq_ref, ysq_ref, a_ref, at_ref, col_ref):
    spread(col_ref, columns_of(xsq_ref[...]), GROUP)

    def some(r, carry):
        for k in range(UNROLL):
            e = r * UNROLL + k
            s = jnp.minimum(table_ref[AT_SRC + e], GROUP - 1)
            t = jnp.minimum(table_ref[AT_TGT + e], GROUP - 1)
            cross = lax.dot_general(
                x_ref[s], y_ref[t], (((1,), (1,)), ((), ())), preferred_element_type=F32
            )
            cost = (col_ref[s] + ysq_ref[pl.ds(t, 1), :] - 2.0 * cross) * scale
            a_ref[e] = cost
            at_ref[e] = cost.T
        return carry

    lax.fori_loop(0, lax.div(table_ref[AT_LIVE] + (UNROLL - 1), UNROLL), some, 0)


def fine_costs(table, x, y, xsq, ysq, scale):
    shape = jax.ShapeDtypeStruct((SLOTS, BLK, BLK), F32)
    return pl.pallas_call(
        functools.partial(fine_cost_kernel, scale),
        out_shape=(shape, shape),
        in_specs=smem(1) + spec(4),
        out_specs=tuple(spec(2)),
        scratch_shapes=[pltpu.VMEM((GROUP, BLK, BLK), F32)],
        name="fine_costs",
    )(table, x, y, xsq, ysq)


def looked_up(coarse_ref, ids_ref, pot_ref):
    rows = coarse_ref.shape[0]
    by_lane = columns_of(coarse_ref[...])[:, :rows]
    high = by_lane.astype(BF16)
    rest = by_lane - high.astype(F32)
    middle = rest.astype(BF16)
    low = (rest - middle.astype(F32)).astype(BF16)
    parts = jnp.concatenate([high, middle, low, jnp.zeros_like(low)], axis=1)
    depth = 4 * rows
    row_at = lax.rem(lax.broadcasted_iota(jnp.int32, (depth, BLK), 0), rows)
    lane_at = lax.broadcasted_iota(jnp.int32, (BLK, BLK), 0)

    def some(r, carry):
        for k in range(UNROLL):
            ids = ids_ref[pl.ds(r * UNROLL + k, 1), :]
            pick = jnp.where(row_at == (ids >> 7), 1.0, 0.0).astype(BF16)
            found = jnp.dot(parts, pick, preferred_element_type=F32)
            pot_ref[pl.ds(r * UNROLL + k, 1), :] = jnp.sum(
                jnp.where(lane_at == (ids & (BLK - 1)), found, 0.0), axis=0, keepdims=True
            )
        return carry

    lax.fori_loop(0, GROUP // UNROLL, some, 0)


def fine_half_kernel(first, given_at, into_at, *refs):
    if first:
        table_ref, coarse_ref, ids_ref, mat_ref, out_ref, col_ref, top_ref, sum_ref = refs
        looked_up(coarse_ref, ids_ref, top_ref)
        potential = top_ref[0:GROUP, :]
    else:
        table_ref, recv_ref, mat_ref, out_ref, col_ref, top_ref, sum_ref = refs
        potential = -joined(recv_ref)
    spread(col_ref, columns_of(potential), GROUP)
    top_ref[...] = jnp.full(top_ref.shape, NEG, F32)
    sum_ref[...] = jnp.zeros(sum_ref.shape, F32)

    def some(r, carry):
        found = []
        for k in range(UNROLL):
            e = r * UNROLL + k
            given = jnp.minimum(table_ref[given_at + e], GROUP - 1)
            rating = (col_ref[given] - mat_ref[e]).reshape(BLK // 8, 8, BLK)
            top = jnp.max(rating, axis=0)
            total = jnp.sum(jnp.exp(rating - top[None]), axis=0)
            best = jnp.max(top, axis=0, keepdims=True)
            found.append((best, jnp.sum(total * jnp.exp(top - best), axis=0, keepdims=True)))
        for k in range(UNROLL):
            into = table_ref[into_at + r * UNROLL + k]
            row = pl.ds(into, 1)
            best, total = found[k]
            before = top_ref[row, :]
            now = jnp.maximum(before, best)
            sum_ref[row, :] = sum_ref[row, :] * jnp.exp(before - now) + total * jnp.exp(best - now)
            top_ref[row, :] = now
        return carry

    lax.fori_loop(0, lax.div(table_ref[AT_LIVE] + (UNROLL - 1), UNROLL), some, 0)
    result = top_ref[0:GROUP, :] + jnp.log(sum_ref[0:GROUP, :])
    for k in range(SIDE):
        out_ref[k] = result


def fine_half(first, given_at, into_at, table, given, mat):
    return pl.pallas_call(
        functools.partial(fine_half_kernel, first, given_at, into_at),
        out_shape=jax.ShapeDtypeStruct((SIDE, GROUP, BLK), F32),
        in_specs=smem(1) + spec(len(given) + 1),
        out_specs=spec(1)[0],
        scratch_shapes=[
            pltpu.VMEM((GROUP, BLK, BLK), F32),
            pltpu.VMEM((GROUP + 8, BLK), F32),
            pltpu.VMEM((GROUP + 8, BLK), F32),
        ],
        compiler_params=pltpu.CompilerParams(vmem_limit_bytes=16 << 20),
        name="fine_half",
    )(table, *given, mat)


def own_kernel(place_ref, srecv_ref, trecv_ref, s_ref, t_ref, sown_ref, town_ref):
    s_ref[...] = -joined(srecv_ref)
    t_ref[...] = -joined(trecv_ref)
    own_s = pl.ds(pl.multiple_of(place_ref[0] * OWN, OWN), OWN)
    own_t = pl.ds(pl.multiple_of(place_ref[1] * OWN, OWN), OWN)
    sown_ref[...] = HEAT * s_ref[own_s, :]
    town_ref[...] = HEAT * t_ref[own_t, :]


def final_potentials(place, srecv, trecv):
    some = jax.ShapeDtypeStruct((GROUP, BLK), F32)
    own = jax.ShapeDtypeStruct((OWN, BLK), F32)
    return pl.pallas_call(
        own_kernel,
        out_shape=(some, some, own, own),
        in_specs=smem(1) + spec(2),
        out_specs=tuple(spec(4)),
        compiler_params=pltpu.CompilerParams(vmem_limit_bytes=4 << 20),
        name="final_potentials",
    )(place, srecv, trecv)


def masses_put(buf, at, mass, width):
    high = mass.astype(BF16).astype(F32)
    both = jnp.concatenate([high, mass - high, jnp.zeros((8, width - 2 * BLK), F32)], axis=1)
    buf[at, HALF * BLK :, :] = jnp.concatenate([both, jnp.zeros_like(both)], axis=0).astype(BF16)


def masses_of(tail):
    return tail[:, 0:BLK].astype(F32) + tail[:, BLK : 2 * BLK].astype(F32)


def sums_kernel(by_src, table_ref, place_ref, picks_ref, mine_ref, other_ref, mat_ref, rows_ref, out_ref, acc_ref, mass_ref):
    q = pl.program_id(0)
    away, half = lax.div(picks_ref[q], 2), lax.rem(picks_ref[q], 2)
    base = lax.rem(place_ref[0 if by_src else 1] + away, SIDE) * OWN + half * HALF
    ones = jnp.ones((8, BLK), BF16)
    partner = AT_TGT if by_src else AT_SRC

    def term(block, k, column, live):
        if by_src:
            e = table_ref[AT_START + block] + k
        else:
            e = table_ref[AT_LIST + block * 16 + k]
        peer = jnp.minimum(table_ref[partner + e], GROUP - 1)
        plan = jnp.exp(column + other_ref[pl.ds(peer, 1), :] - mat_ref[e])
        if live is not None:
            plan = jnp.where(live, plan, 0.0)
        plan = plan.astype(BF16)
        total = jnp.dot(plan, rows_ref[peer], preferred_element_type=F32)
        mass = lax.dot_general(ones, plan, (((1,), (1,)), ((), ())), preferred_element_type=F32)
        return total, mass[0:1, :]

    columns, counts = [], []
    for b in range(HALF):
        block = base + b
        if by_src:
            count = table_ref[AT_START + block + 1] - table_ref[AT_START + block]
        else:
            count = table_ref[AT_COUNT + block]
        column = jnp.broadcast_to(mine_ref[pl.ds(block, 1), :], (BLK, BLK)).T
        total, mass = term(block, 0, column, count > 0)
        acc_ref[b] = total
        mass_ref[b : b + 1, :] = mass
        counts.append(count)
    for b in range(HALF):

        def more(k, carry, b=b):
            column = jnp.broadcast_to(mine_ref[pl.ds(base + b, 1), :], (BLK, BLK)).T
            total, mass = term(base + b, k, column, None)
            acc_ref[b] += total
            mass_ref[b : b + 1, :] += mass
            return carry

        lax.fori_loop(1, counts[b], more, 0)
    for b in range(HALF):
        out_ref[0, b * BLK : (b + 1) * BLK, :] = acc_ref[b].astype(BF16)
    masses_put(out_ref, 0, mass_ref[...], out_ref.shape[2])


def weighted_sums(by_src, picks, table, place, mine, other, mat, rows):
    width = rows.shape[2]
    return pl.pallas_call(
        functools.partial(sums_kernel, by_src),
        out_shape=jax.ShapeDtypeStruct((len(picks), HALF_ROWS, width), BF16),
        grid=(len(picks),),
        in_specs=smem(3) + spec(4),
        out_specs=pl.BlockSpec((1, HALF_ROWS, width), lambda q: (q, 0, 0)),
        scratch_shapes=[pltpu.VMEM((HALF, BLK, width), F32), pltpu.VMEM((8, BLK), F32)],
        compiler_params=pltpu.CompilerParams(vmem_limit_bytes=24 << 20),
        name="weighted_sums",
    )(table, place, jnp.array(picks, jnp.int32), mine, other, mat, rows)


def add_kernel(a_ref, b_ref, out_ref):
    for b in range(HALF):
        rows = slice(b * BLK, (b + 1) * BLK)
        out_ref[0, rows, :] = (a_ref[0, rows, :].astype(F32) + b_ref[0, rows, :].astype(F32)).astype(BF16)
    tail = slice(HALF * BLK, HALF_ROWS)
    mass = masses_of(a_ref[0, tail, :]) + masses_of(b_ref[0, tail, :])
    masses_put(out_ref, 0, mass[0:8, :], out_ref.shape[2])


def added(a, b):
    return pl.pallas_call(
        add_kernel,
        out_shape=jax.ShapeDtypeStruct(a.shape, BF16),
        in_specs=spec(2),
        out_specs=spec(1)[0],
        compiler_params=pltpu.CompilerParams(vmem_limit_bytes=8 << 20),
        name="added",
    )(a, b)


def mean_kernel(*refs):
    ins, out_ref = refs[:-1], refs[-1]
    step = pl.program_id(0)

    def give(rows, tails, b):
        mass = masses_of(tails[0][0])
        total = rows[0][0].astype(F32)
        for row, tail in zip(rows[1:], tails[1:]):
            mass = mass + masses_of(tail[0])
            total = total + row[0].astype(F32)
        pick = lax.broadcasted_iota(jnp.int32, mass.shape, 0) == b
        line = jnp.sum(jnp.where(pick, mass, 0.0), axis=0, keepdims=True)
        share = jnp.broadcast_to(1.0 / line, (BLK, BLK)).T
        out_ref[...] = (total * share[:, 0:1]).astype(BF16)

    @pl.when(step < HALF)
    def _():
        give(ins[0:3], ins[6:9], step)

    @pl.when(step >= HALF)
    def _():
        give(ins[3:6], ins[9:12], step - HALF)


def mean_of(low, high):
    width = low[0][0].shape[2]
    loads, rows, tails = [], [], []
    for group, at in ((low, lambda b: jnp.minimum(b, HALF - 1)), (high, lambda b: jnp.maximum(b - HALF, 0))):
        for array, row in group:
            loads.append(array)
            rows.append(pl.BlockSpec((1, BLK, width), lambda b, row=row, at=at: (row, at(b), 0)))
            tails.append(pl.BlockSpec((1, 16, width), lambda b, row=row: (row, HALF * BLK // 16, 0)))
    return pl.pallas_call(
        mean_kernel,
        out_shape=jax.ShapeDtypeStruct((OWN * BLK, width), BF16),
        grid=(OWN,),
        in_specs=rows + tails,
        out_specs=pl.BlockSpec((BLK, width), lambda b: (b, 0)),
        compiler_params=pltpu.CompilerParams(vmem_limit_bytes=16 << 20),
        name="mean_of",
    )(*loads, *loads)


NARROW = ("y", "x")


def exchanged(copies, axis):
    return lax.all_to_all(copies, axis, split_axis=0, concat_axis=0, tiled=True)


def copied(value, axis):
    count = lax.axis_size(axis) if isinstance(axis, str) else SIDE * SIDE
    return exchanged(jnp.broadcast_to(value, (count, *value.shape)), axis)


def shifted(value, axis, away):
    return lax.ppermute(value, axis, [(k, (k + away) % SIDE) for k in range(SIDE)])


def far_sent(far, axis):
    return shifted(far[0:1], axis, 1), shifted(far[1:2], axis, -1)


def near_sent(near, far_low, far_high, axis):
    plain_high = shifted(near[2:3], axis, 1)
    plain_low = shifted(near[3:4], axis, -1)
    sum_low = shifted(added(far_low, near[0:1]), axis, 1)
    sum_high = shifted(added(far_high, near[1:2]), axis, -1)
    low = [(near, 4), (plain_low, 0), (sum_low, 0)]
    high = [(near, 5), (plain_high, 0), (sum_high, 0)]
    return low, high


def beside_core(value):
    return lax.ppermute(value, "wide", [(k, k ^ 1) for k in range(2 * SIDE)])


def along_z(value, away):
    ring = [(k, (k // 2 + away) % SIDE * 2 + k % 2) for k in range(2 * SIDE)]
    return lax.ppermute(value, "wide", ring)


def square_norms(rows):
    return jnp.sum(jnp.square(rows.astype(F32)), axis=-1)


def body(
    sources,
    targets,
    target_lists,
    target_clusters,
    centroids_src,
    centroids_tgt,
    sender_mean_measure,
    recipient_mean_measure,
):
    width = sources.shape[1]
    wide = lax.axis_size("wide")
    narrow = SIDE * SIDE
    scale = 1.0 / (width * HEAT)
    y, x = lax.axis_index("y"), lax.axis_index("x")
    w = lax.axis_index("wide")
    place = jnp.stack([y, x, w // 2, w % 2]).astype(jnp.int32)

    cols = centroids_tgt.T
    cols = jnp.stack([cols, beside_core(cols)])
    cols = [cols] + [along_z(cols, away) for away in range(1, SIDE)]
    rows = copied(centroids_src, NARROW).reshape(-1, width)

    facts = jnp.concatenate(
        [
            jnp.pad(target_lists.reshape(1, -1).astype(F32), ((0, 0), (0, BLK - OWN * LIST))),
            target_clusters.reshape(OWN, BLK).astype(F32),
            square_norms(sources).reshape(OWN, BLK),
            square_norms(targets).reshape(OWN, BLK),
        ],
        axis=0,
    )
    facts = copied(facts, NARROW).reshape(SIDE, SIDE, LINES, BLK)
    of_column = lax.dynamic_index_in_dim(facts, x, axis=1, keepdims=False)
    of_row = lax.dynamic_index_in_dim(facts, y, axis=0, keepdims=False)
    lists = of_column[:, 0, : OWN * LIST].astype(jnp.int32).reshape(-1)
    ids = of_row[:, 1 : 1 + OWN].astype(jnp.int32).reshape(GROUP, BLK)
    src_sq = of_column[:, 1 + OWN : 1 + 2 * OWN].reshape(GROUP, BLK)
    tgt_sq = of_row[:, 1 + 2 * OWN :].reshape(GROUP, BLK)
    table = entry_table(lists, place)

    rows, sources, targets = lax.optimization_barrier((rows, sources, targets))
    all_targets = lax.all_gather(targets, "x", axis=0).reshape(GROUP, BLK, width)
    all_sources = lax.all_gather(sources, "y", axis=0).reshape(GROUP, BLK, width)

    by_col, by_row = coarse_costs(place, rows, cols, scale)
    row_mass = sender_mean_measure.reshape(-1, BLK)
    col_mass = recipient_mean_measure.reshape(-1, BLK)
    recv = jnp.zeros((wide, *col_mass.shape), F32)
    for turn in range(ITC):
        sent = coarse_half(turn == 0, recv, col_mass, by_row, narrow)
        sent = coarse_half(False, exchanged(sent, NARROW), row_mass, by_col, wide)
        recv = exchanged(sent, "wide")
        if turn == ITC - 3:
            recv, table = lax.optimization_barrier((recv, table))
        if turn == ITC - 2:
            a, at = fine_costs(table, all_sources, all_targets, src_sq, tgt_sq, scale)
            recv, a, at = lax.optimization_barrier((recv, a, at))
    coarse = exchanged(coarse_end(recv, col_mass, narrow), NARROW).reshape(-1, BLK)

    given, first = (coarse, ids), True
    for step in range(STEPS):
        src_parts = exchanged(fine_half(first, AT_TGT, AT_SRC, table, given, at), "y")
        tgt_parts = exchanged(fine_half(False, AT_SRC, AT_TGT, table, (src_parts,), a), "x")
        given, first = (tgt_parts,), False

    s_pot, t_pot, s_own, t_own = final_potentials(place, src_parts, tgt_parts)
    src_args = (table, place, s_pot, t_pot, a, all_targets)
    tgt_args = (table, place, t_pot, s_pot, at, all_sources)
    src_far = far_sent(weighted_sums(True, FAR, *src_args), "y")
    tgt_far = far_sent(weighted_sums(False, FAR, *tgt_args), "x")
    src_near = weighted_sums(True, NEAR, *src_args)
    tgt_near = weighted_sums(False, NEAR, *tgt_args)
    src_mean = mean_of(*near_sent(src_near, *src_far, "y"))
    tgt_mean = mean_of(*near_sent(tgt_near, *tgt_far, "x"))
    return src_mean, tgt_mean, s_own.reshape(-1), t_own.reshape(-1)


def solution(mesh):
    wide, narrow = (mesh.shape[axis] for axis in ("wide", "narrow"))
    devices = mesh.devices.reshape(wide, SIDE, narrow // SIDE)
    grid = Mesh(devices, ("wide", "y", "x"))
    everyone = ("wide", "y", "x")
    in_specs = (
        P(everyone, None),
        P(everyone, None),
        P(everyone, None),
        P(everyone),
        P(everyone, None),
        P(NARROW, "wide"),
        P("wide"),
        P(NARROW),
    )
    out_specs = (P(everyone, None), P(everyone, None), P(everyone), P(everyone))
    return jax.shard_map(body, mesh=grid, in_specs=in_specs, out_specs=out_specs, check_vma=False)
```

```python
import functools

import jax
import jax.numpy as jnp
from jax import lax
from jax.experimental import pallas as pl
from jax.experimental.pallas import tpu as pltpu
from jax.sharding import Mesh
from jax.sharding import PartitionSpec as P

BLK = 128
LIST = 4
ITC = 6
STEPS = 3
CAP = 3
HEAT = 0.02
SIDE = 4
OWN = 8
GROUP = SIDE * OWN
UNROLL = 4
SLOTS = SIDE * SIDE * CAP + UNROLL
HALF = OWN // 2
HALF_ROWS = HALF * BLK + 16
FAR, PLAIN, JOINT, HOME = (4, 5), (6, 3), (2, 7), (0, 1)
NEG = -1e30
AT_SRC, AT_TGT, AT_START, AT_COUNT, AT_LIST, AT_LIVE, TABLE = 0, 64, 128, 168, 200, 712, 768
LINES = 3 * OWN + 1

F32 = jnp.float32
BF16 = jnp.bfloat16


def spec(n):
    return [pl.BlockSpec(memory_space=pltpu.VMEM)] * n


def smem(n):
    return [pl.BlockSpec(memory_space=pltpu.SMEM)] * n


def columns_of(rows):
    count = rows.shape[0]
    if count < BLK:
        rows = jnp.concatenate([rows, jnp.zeros((BLK - count, BLK), F32)], axis=0)
    return rows.T


def spread(col_ref, columns, count):
    for k in range(count):
        col_ref[k] = jnp.broadcast_to(columns[:, k : k + 1], (BLK, BLK))


def joined(parts_ref, rows=None):
    parts = [parts_ref[k, 0:rows, :] for k in range(parts_ref.shape[0])]
    top = tree(parts, jnp.maximum)
    return top + jnp.log(tree([jnp.exp(part - top) for part in parts], jnp.add))


def tree(parts, op):
    while len(parts) > 1:
        parts = [op(a, b) for a, b in zip(parts[::2], parts[1::2])] + (
            [parts[-1]] if len(parts) % 2 else []
        )
    return parts[0]


def coarse_cost_kernel(scale, place_ref, x_ref, *refs):
    pieces, (by_col_ref, by_row_ref, y_ref, ysq_ref) = refs[:SIDE], refs[SIDE:]
    z, core = place_ref[2], place_ref[3]
    depth, cols = pieces[0].shape[1], y_ref.shape[1] // BLK
    for away in range(SIDE):
        home = lax.rem(z + SIDE - away, SIDE) * 2
        for twin in range(2):
            at = (home + lax.rem(core + twin, 2)) * depth
            y_ref[pl.ds(pl.multiple_of(at, depth), depth), :] = pieces[away][twin]
    for k in range(cols):
        wide_y = y_ref[:, k * BLK : (k + 1) * BLK].astype(F32)
        ysq_ref[k : k + 1, :] = jnp.sum(wide_y * wide_y, axis=0, keepdims=True)
    tall = 2 * BLK

    def one(j, carry):
        x = x_ref[pl.ds(pl.multiple_of(j * tall, tall), tall), :]
        wide_x = x.astype(F32)
        x_sq = jnp.sum(wide_x * wide_x, axis=1, keepdims=True)
        for k in range(cols):
            y = y_ref[:, k * BLK : (k + 1) * BLK]
            cross = jnp.dot(x, y, preferred_element_type=F32)
            cost = (x_sq + ysq_ref[k : k + 1, :] - 2.0 * cross) * scale
            by_col_ref[k, pl.ds(pl.multiple_of(j * tall, tall), tall), :] = cost
            for h in range(2):
                by_row_ref[2 * j + h, k * BLK : (k + 1) * BLK, :] = cost[
                    h * BLK : (h + 1) * BLK, :
                ].T
        return carry

    lax.fori_loop(0, x_ref.shape[0] // tall, one, 0)


def coarse_costs(place, x, pieces, scale):
    rows, cols = x.shape[0] // BLK, pieces[0].shape[2] // BLK
    return pl.pallas_call(
        functools.partial(coarse_cost_kernel, scale),
        out_shape=(
            jax.ShapeDtypeStruct((cols, rows * BLK, BLK), F32),
            jax.ShapeDtypeStruct((rows, cols * BLK, BLK), F32),
        ),
        in_specs=smem(1) + spec(1 + SIDE),
        out_specs=tuple(spec(2)),
        scratch_shapes=[
            pltpu.VMEM((x.shape[1], cols * BLK), BF16),
            pltpu.VMEM((8, BLK), F32),
        ],
        compiler_params=pltpu.CompilerParams(vmem_limit_bytes=20 << 20),
        name="coarse_costs",
    )(place, x, *pieces)


def coarse_half_kernel(first, recv_ref, mass_ref, cost_ref, out_ref, col_ref, res_ref):
    given = mass_ref.shape[0]
    chunks = cost_ref.shape[0]
    if first:
        potential = jnp.zeros((given, BLK), F32)
    else:
        potential = jnp.log(mass_ref[...]) - joined(recv_ref, given)
    spread(col_ref, columns_of(potential), given)

    def chunk(c, carry):
        def piece(k):
            cost = cost_ref[c, k * BLK : (k + 1) * BLK, :]
            return (col_ref[k] - cost).reshape(BLK // 8, 8, BLK)

        top = tree([jnp.max(piece(k), axis=0) for k in range(given)], jnp.maximum)
        total = tree(
            [jnp.sum(jnp.exp(piece(k) - top[None]), axis=0) for k in range(given)], jnp.add
        )
        best = jnp.max(top, axis=0, keepdims=True)
        total = jnp.sum(total * jnp.exp(top - best), axis=0, keepdims=True)
        res_ref[pl.ds(c, 1), :] = best + jnp.log(total)
        return carry

    lax.fori_loop(0, chunks, chunk, 0)
    result = res_ref[0:chunks, :]
    for k in range(out_ref.shape[0]):
        out_ref[k, 0:chunks, :] = result
        if first:
            out_ref[k, chunks:, :] = recv_ref[...]


def coarse_half(first, recv, mass, cost, copies):
    given, chunks = mass.shape[0], cost.shape[0]
    lines = chunks + (recv.shape[0] if first else 0)
    return pl.pallas_call(
        functools.partial(coarse_half_kernel, first),
        out_shape=jax.ShapeDtypeStruct((copies, lines, BLK), F32),
        in_specs=spec(3),
        out_specs=spec(1)[0],
        scratch_shapes=[pltpu.VMEM((given, BLK, BLK), F32), pltpu.VMEM((8, BLK), F32)],
        compiler_params=pltpu.CompilerParams(vmem_limit_bytes=12 << 20),
        name="coarse_half",
    )(recv, mass, cost)


def coarse_end_kernel(recv_ref, mass_ref, out_ref):
    potential = jnp.log(mass_ref[...]) - joined(recv_ref)
    for k in range(out_ref.shape[0]):
        out_ref[k] = potential


def coarse_end(recv, mass, copies):
    return pl.pallas_call(
        coarse_end_kernel,
        out_shape=jax.ShapeDtypeStruct((copies, *mass.shape), F32),
        in_specs=spec(2),
        out_specs=spec(1)[0],
        name="coarse_end",
    )(recv, mass)


def plan_kernel(lists_ref, place_ref, table_ref):
    y = place_ref[0]

    def clear(k, carry):
        for j in range(8):
            table_ref[k * 8 + j] = 0
        return carry

    lax.fori_loop(0, TABLE // 8, clear, 0)

    def scan(q, live):
        block = lists_ref[q]
        device = lax.rem(lax.div(block, OWN), SIDE * SIDE)
        here = (lax.div(device, SIDE) == y).astype(jnp.int32)
        s = lax.div(q, LIST)
        t = lax.rem(device, SIDE) * OWN + lax.rem(block, OWN)
        table_ref[AT_SRC + live] = s
        table_ref[AT_TGT + live] = t
        seen = table_ref[AT_COUNT + t]
        table_ref[AT_LIST + t * 16 + seen] = live
        table_ref[AT_COUNT + t] = seen + here
        live = live + here
        table_ref[AT_START + s + 1] = live
        return live

    live = lax.fori_loop(0, SIDE * OWN * LIST, scan, 0)
    for k in range(UNROLL + 1):
        table_ref[AT_SRC + live + k] = GROUP
        table_ref[AT_TGT + live + k] = GROUP
    table_ref[AT_LIVE] = live


def entry_table(lists, place):
    return pl.pallas_call(
        plan_kernel,
        out_shape=jax.ShapeDtypeStruct((TABLE,), jnp.int32),
        in_specs=smem(2),
        out_specs=smem(1)[0],
        name="entry_table",
    )(lists, place)


def fine_cost_kernel(scale, table_ref, x_ref, y_ref, xsq_ref, ysq_ref, a_ref, at_ref, col_ref):
    spread(col_ref, columns_of(xsq_ref[...]), GROUP)

    def some(r, carry):
        for k in range(UNROLL):
            e = r * UNROLL + k
            s = jnp.minimum(table_ref[AT_SRC + e], GROUP - 1)
            t = jnp.minimum(table_ref[AT_TGT + e], GROUP - 1)
            cross = lax.dot_general(
                x_ref[s], y_ref[t], (((1,), (1,)), ((), ())), preferred_element_type=F32
            )
            cost = (col_ref[s] + ysq_ref[pl.ds(t, 1), :] - 2.0 * cross) * scale
            a_ref[e] = cost
            at_ref[e] = cost.T
        return carry

    lax.fori_loop(0, lax.div(table_ref[AT_LIVE] + (UNROLL - 1), UNROLL), some, 0)


def fine_costs(table, x, y, xsq, ysq, scale):
    shape = jax.ShapeDtypeStruct((SLOTS, BLK, BLK), F32)
    return pl.pallas_call(
        functools.partial(fine_cost_kernel, scale),
        out_shape=(shape, shape),
        in_specs=smem(1) + spec(4),
        out_specs=tuple(spec(2)),
        scratch_shapes=[pltpu.VMEM((GROUP, BLK, BLK), F32)],
        compiler_params=pltpu.CompilerParams(vmem_limit_bytes=24 << 20),
        name="fine_costs",
    )(table, x, y, xsq, ysq)


def looked_up(coarse_ref, ids_ref, pot_ref):
    rows = coarse_ref.shape[0]
    by_lane = columns_of(coarse_ref[...])[:, :rows]
    high = by_lane.astype(BF16)
    rest = by_lane - high.astype(F32)
    middle = rest.astype(BF16)
    low = (rest - middle.astype(F32)).astype(BF16)
    parts = jnp.concatenate([high, middle, low, jnp.zeros_like(low)], axis=1)
    depth = 4 * rows
    row_at = lax.rem(lax.broadcasted_iota(jnp.int32, (depth, BLK), 0), rows)
    lane_at = lax.broadcasted_iota(jnp.int32, (BLK, BLK), 0)

    def some(r, carry):
        for k in range(UNROLL):
            ids = ids_ref[pl.ds(r * UNROLL + k, 1), :]
            pick = jnp.where(row_at == (ids >> 7), 1.0, 0.0).astype(BF16)
            found = jnp.dot(parts, pick, preferred_element_type=F32)
            pot_ref[pl.ds(r * UNROLL + k, 1), :] = jnp.sum(
                jnp.where(lane_at == (ids & (BLK - 1)), found, 0.0), axis=0, keepdims=True
            )
        return carry

    lax.fori_loop(0, GROUP // UNROLL, some, 0)


def fine_half_kernel(first, last, given_at, into_at, *refs):
    *refs, col_ref, top_ref, sum_ref = refs
    if last:
        *refs, pot_ref = refs
    if first:
        table_ref, coarse_ref, ids_ref, mat_ref, out_ref = refs
        looked_up(coarse_ref, ids_ref, top_ref)
        potential = top_ref[0:GROUP, :]
    else:
        table_ref, recv_ref, mat_ref, out_ref = refs
        potential = -joined(recv_ref)
    if last:
        pot_ref[...] = potential
    spread(col_ref, columns_of(potential), GROUP)
    top_ref[...] = jnp.full(top_ref.shape, NEG, F32)
    sum_ref[...] = jnp.zeros(sum_ref.shape, F32)

    def some(r, carry):
        found = []
        for k in range(UNROLL):
            e = r * UNROLL + k
            given = jnp.minimum(table_ref[given_at + e], GROUP - 1)
            rating = (col_ref[given] - mat_ref[e]).reshape(BLK // 8, 8, BLK)
            top = jnp.max(rating, axis=0)
            total = jnp.sum(jnp.exp(rating - top[None]), axis=0)
            best = jnp.max(top, axis=0, keepdims=True)
            found.append((best, jnp.sum(total * jnp.exp(top - best), axis=0, keepdims=True)))
        for k in range(UNROLL):
            into = table_ref[into_at + r * UNROLL + k]
            row = pl.ds(into, 1)
            best, total = found[k]
            before = top_ref[row, :]
            now = jnp.maximum(before, best)
            sum_ref[row, :] = sum_ref[row, :] * jnp.exp(before - now) + total * jnp.exp(best - now)
            top_ref[row, :] = now
        return carry

    lax.fori_loop(0, lax.div(table_ref[AT_LIVE] + (UNROLL - 1), UNROLL), some, 0)
    result = top_ref[0:GROUP, :] + jnp.log(sum_ref[0:GROUP, :])
    for k in range(SIDE):
        out_ref[k] = result


def fine_half(first, last, given_at, into_at, table, given, mat):
    shapes = (
        jax.ShapeDtypeStruct((SIDE, GROUP, BLK), F32),
        jax.ShapeDtypeStruct((GROUP, BLK), F32),
    )
    return pl.pallas_call(
        functools.partial(fine_half_kernel, first, last, given_at, into_at),
        out_shape=shapes if last else shapes[0],
        in_specs=smem(1) + spec(len(given) + 1),
        out_specs=tuple(spec(2)) if last else spec(1)[0],
        scratch_shapes=[
            pltpu.VMEM((GROUP, BLK, BLK), F32),
            pltpu.VMEM((GROUP + 8, BLK), F32),
            pltpu.VMEM((GROUP + 8, BLK), F32),
        ],
        compiler_params=pltpu.CompilerParams(vmem_limit_bytes=16 << 20),
        name="fine_half",
    )(table, *given, mat)


def own_kernel(place_ref, s_ref, trecv_ref, t_ref, sown_ref, town_ref, share_ref):
    y, x = place_ref[0], place_ref[1]
    t_ref[...] = -joined(trecv_ref)

    def owned(device):
        return pl.ds(pl.multiple_of(device * OWN, OWN), OWN)

    sown_ref[...] = HEAT * s_ref[owned(y), :]
    town_ref[...] = HEAT * t_ref[owned(x), :]
    after, before = lax.rem(x + 1, SIDE), lax.rem(x + SIDE - 1, SIDE)
    for k, (sender, owner) in enumerate(((before, after), (after, before))):
        share = jnp.exp(trecv_ref[sender, owned(owner), :] + t_ref[owned(owner), :])
        share_ref[k, 0:HALF, :] = share[k * HALF : (k + 1) * HALF, :]
        share_ref[k, HALF:, :] = jnp.zeros((OWN - HALF, BLK), F32)


def final_potentials(place, s_pot, trecv):
    some = jax.ShapeDtypeStruct((GROUP, BLK), F32)
    own = jax.ShapeDtypeStruct((OWN, BLK), F32)
    return pl.pallas_call(
        own_kernel,
        out_shape=(some, own, own, jax.ShapeDtypeStruct((2, OWN, BLK), F32)),
        in_specs=smem(1) + spec(2),
        out_specs=tuple(spec(4)),
        compiler_params=pltpu.CompilerParams(vmem_limit_bytes=4 << 20),
        name="final_potentials",
    )(place, s_pot, trecv)


def masses_put(buf, mass):
    width = buf.shape[1]
    high = mass.astype(BF16).astype(F32)
    both = jnp.concatenate([high, mass - high, jnp.zeros((8, width - 2 * BLK), F32)], axis=1)
    buf[HALF * BLK :, :] = jnp.concatenate([both, jnp.zeros_like(both)], axis=0).astype(BF16)


def masses_of(tail):
    return tail[:, 0:BLK].astype(F32) + tail[:, BLK : 2 * BLK].astype(F32)


def sums_kernel(by_src, table_ref, place_ref, picks_ref, mine_ref, other_ref, mat_ref, rows_ref, *refs):
    *out_refs, acc_ref, mass_ref = refs
    q = pl.program_id(0)
    away, half = lax.div(picks_ref[q], 2), lax.rem(picks_ref[q], 2)
    base = lax.rem(place_ref[0 if by_src else 1] + away, SIDE) * OWN + half * HALF
    ones = jnp.ones((8, BLK), BF16)
    partner = AT_TGT if by_src else AT_SRC

    def term(block, k, column, live):
        if by_src:
            e = table_ref[AT_START + block] + k
        else:
            e = table_ref[AT_LIST + block * 16 + k]
        peer = jnp.minimum(table_ref[partner + e], GROUP - 1)
        plan = jnp.exp(column + other_ref[pl.ds(peer, 1), :] - mat_ref[e])
        if live is not None:
            plan = jnp.where(live, plan, 0.0)
        plan = plan.astype(BF16)
        total = jnp.dot(plan, rows_ref[peer], preferred_element_type=F32)
        mass = lax.dot_general(ones, plan, (((1,), (1,)), ((), ())), preferred_element_type=F32)
        return total, mass[0:1, :]

    def column_of(block):
        if len(mine_ref.shape) == 3:
            line = -mine_ref[0, pl.ds(block, 1), :]
        else:
            line = mine_ref[pl.ds(block, 1), :]
        return jnp.broadcast_to(line, (BLK, BLK)).T

    counts = []
    for b in range(HALF):
        block = base + b
        if by_src:
            count = table_ref[AT_START + block + 1] - table_ref[AT_START + block]
        else:
            count = table_ref[AT_COUNT + block]
        total, mass = term(block, 0, column_of(block), count > 0)
        acc_ref[b] = total
        mass_ref[b : b + 1, :] = mass
        counts.append(count)
    for b in range(HALF):

        def more(k, carry, b=b):
            total, mass = term(base + b, k, column_of(base + b), None)
            acc_ref[b] += total
            mass_ref[b : b + 1, :] += mass
            return carry

        lax.fori_loop(1, counts[b], more, 0)
    for k, out_ref in enumerate(out_refs):

        @pl.when(q == k)
        def _(out_ref=out_ref):
            for b in range(HALF):
                out_ref[b * BLK : (b + 1) * BLK, :] = acc_ref[b].astype(BF16)
            masses_put(out_ref, mass_ref[...])


def weighted_sums(by_src, picks, table, place, mine, other, mat, rows):
    width = rows.shape[2]
    return pl.pallas_call(
        functools.partial(sums_kernel, by_src),
        out_shape=(jax.ShapeDtypeStruct((HALF_ROWS, width), BF16),) * len(picks),
        grid=(len(picks),),
        in_specs=smem(3) + spec(4),
        out_specs=tuple(spec(len(picks))),
        scratch_shapes=[pltpu.VMEM((HALF, BLK, width), F32), pltpu.VMEM((8, BLK), F32)],
        compiler_params=pltpu.CompilerParams(vmem_limit_bytes=16 << 20),
        name="weighted_sums",
    )(table, place, jnp.array(picks, jnp.int32), mine, other, mat, rows)


def add_kernel(which, a_ref, b_ref, *refs):
    out_ref = refs[-1]
    tail = slice(HALF * BLK, HALF_ROWS)
    mass = masses_of(a_ref[tail, :])[0:OWN, :]
    if which is not None:
        mass = mass * refs[0][which]
    for b in range(HALF):
        rows = slice(b * BLK, (b + 1) * BLK)
        total = a_ref[rows, :].astype(F32)
        if which is not None:
            total = total * jnp.broadcast_to(refs[0][which, b : b + 1, :], (BLK, BLK)).T[:, 0:1]
        out_ref[rows, :] = (total + b_ref[rows, :].astype(F32)).astype(BF16)
    masses_put(out_ref, mass + masses_of(b_ref[tail, :])[0:OWN, :])


def added(a, b, which, shares):
    given = () if shares is None else (shares,)
    return pl.pallas_call(
        functools.partial(add_kernel, None if shares is None else which),
        out_shape=jax.ShapeDtypeStruct(a.shape, BF16),
        in_specs=spec(2 + len(given)),
        out_specs=spec(1)[0],
        compiler_params=pltpu.CompilerParams(vmem_limit_bytes=8 << 20),
        name="added",
    )(a, b, *given)


def mean_kernel(*refs):
    ins, out_ref = refs[:-1], refs[-1]
    step = pl.program_id(0)

    def give(rows, tails, b):
        mass = masses_of(tails[0])
        total = rows[0][...].astype(F32)
        for row, tail in zip(rows[1:], tails[1:]):
            mass = mass + masses_of(tail)
            total = total + row[...].astype(F32)
        pick = lax.broadcasted_iota(jnp.int32, mass.shape, 0) == b
        line = jnp.sum(jnp.where(pick, mass, 0.0), axis=0, keepdims=True)
        share = jnp.broadcast_to(1.0 / line, (BLK, BLK)).T
        out_ref[...] = (total * share[:, 0:1]).astype(BF16)

    @pl.when(step < HALF)
    def _():
        give(ins[0:3], ins[6:9], step)

    @pl.when(step >= HALF)
    def _():
        give(ins[3:6], ins[9:12], step - HALF)


def mean_of(low, high):
    width = low[0].shape[1]
    loads, rows, tails = [*low, *high], [], []
    for at in (lambda b: jnp.minimum(b, HALF - 1), lambda b: jnp.maximum(b - HALF, 0)):
        rows += [pl.BlockSpec((BLK, width), lambda b, at=at: (at(b), 0))] * 3
        tails += [pl.BlockSpec((16, width), lambda b: (HALF * BLK // 16, 0))] * 3
    return pl.pallas_call(
        mean_kernel,
        out_shape=jax.ShapeDtypeStruct((OWN * BLK, width), BF16),
        grid=(OWN,),
        in_specs=rows + tails,
        out_specs=pl.BlockSpec((BLK, width), lambda b: (b, 0)),
        compiler_params=pltpu.CompilerParams(vmem_limit_bytes=16 << 20),
        name="mean_of",
    )(*loads, *loads)


NARROW = ("y", "x")


def exchanged(copies, axis):
    return lax.all_to_all(copies, axis, split_axis=0, concat_axis=0, tiled=True)


def copied(value, axis):
    count = lax.axis_size(axis) if isinstance(axis, str) else SIDE * SIDE
    return exchanged(jnp.broadcast_to(value, (count, *value.shape)), axis)


def shifted(value, axis, away):
    return lax.ppermute(value, axis, [(k, (k + away) % SIDE) for k in range(SIDE)])


def far_sent(far, axis):
    return shifted(far[0], axis, 1), shifted(far[1], axis, -1)


def plain_sent(plain, axis):
    return shifted(plain[0], axis, -1), shifted(plain[1], axis, 1)


def joint_sent(joint, far, axis, shares=None):
    low = shifted(added(far[0], joint[0], 0, shares), axis, 1)
    return low, shifted(added(far[1], joint[1], 1, shares), axis, -1)


def beside_core(value):
    return lax.ppermute(value, "wide", [(k, k ^ 1) for k in range(2 * SIDE)])


def along_z(value, away):
    ring = [(k, (k // 2 + away) % SIDE * 2 + k % 2) for k in range(2 * SIDE)]
    return lax.ppermute(value, "wide", ring)


def unpacked(facts, place):
    facts = facts.reshape(SIDE, SIDE, LINES, BLK)
    of_column = lax.dynamic_index_in_dim(facts, place[1], axis=1, keepdims=False)
    of_row = lax.dynamic_index_in_dim(facts, place[0], axis=0, keepdims=False)
    lists = of_column[:, 0, : OWN * LIST].astype(jnp.int32).reshape(-1)
    ids = of_row[:, 1 : 1 + OWN].astype(jnp.int32).reshape(GROUP, BLK)
    src_sq = of_column[:, 1 + OWN : 1 + 2 * OWN].reshape(GROUP, BLK)
    tgt_sq = of_row[:, 1 + 2 * OWN :].reshape(GROUP, BLK)
    return entry_table(lists, place), ids, src_sq, tgt_sq


def square_norms(rows):
    return jnp.sum(jnp.square(rows.astype(F32)), axis=-1)


def body(
    sources,
    targets,
    target_lists,
    target_clusters,
    centroids_src,
    centroids_tgt,
    sender_mean_measure,
    recipient_mean_measure,
):
    width = sources.shape[1]
    wide = lax.axis_size("wide")
    narrow = SIDE * SIDE
    scale = 1.0 / (width * HEAT)
    y, x = lax.axis_index("y"), lax.axis_index("x")
    w = lax.axis_index("wide")
    place = jnp.stack([y, x, w // 2, w % 2]).astype(jnp.int32)

    rows = copied(centroids_src, NARROW).reshape(-1, width)
    cols = centroids_tgt.T
    cols = jnp.stack([cols, beside_core(cols)])
    cols = [cols] + [along_z(cols, away) for away in range(1, SIDE)]

    facts = jnp.concatenate(
        [
            jnp.pad(target_lists.reshape(1, -1).astype(F32), ((0, 0), (0, BLK - OWN * LIST))),
            target_clusters.reshape(OWN, BLK).astype(F32),
            square_norms(sources).reshape(OWN, BLK),
            square_norms(targets).reshape(OWN, BLK),
        ],
        axis=0,
    )
    rows, cols, facts, sources, targets = lax.optimization_barrier(
        (rows, cols, facts, sources, targets)
    )
    all_targets = lax.all_gather(targets, "x", axis=0).reshape(GROUP, BLK, width)
    all_sources = lax.all_gather(sources, "y", axis=0).reshape(GROUP, BLK, width)

    by_col, by_row = coarse_costs(place, rows, cols, scale)
    row_mass = sender_mean_measure.reshape(-1, BLK)
    col_mass = recipient_mean_measure.reshape(-1, BLK)
    recv = facts
    for turn in range(ITC):
        sent = coarse_half(turn == 0, recv, col_mass, by_row, narrow)
        got = exchanged(sent, NARROW)
        sent = coarse_half(False, got, row_mass, by_col, wide)
        if turn == 0:
            sent, got = lax.optimization_barrier((sent, got))
            table, ids, src_sq, tgt_sq = unpacked(got[:, OWN:], place)
            recv = exchanged(sent, "wide")
            recv, table, ids, src_sq, tgt_sq = lax.optimization_barrier((recv, table, ids, src_sq, tgt_sq))
        else:
            recv = exchanged(sent, "wide")
    sent = coarse_end(recv, col_mass, narrow)
    sent, table = lax.optimization_barrier((sent, table))
    a, at = fine_costs(table, all_sources, all_targets, src_sq, tgt_sq, scale)
    coarse = exchanged(sent, NARROW).reshape(-1, BLK)

    given, first = (coarse, ids), True
    for step in range(STEPS):
        last = step == STEPS - 1
        sent = fine_half(first, False, AT_TGT, AT_SRC, table, given, at)
        src_parts = exchanged(sent, "y")
        sent = fine_half(False, last, AT_SRC, AT_TGT, table, (src_parts,), a)
        sent, s_pot = sent if last else (sent, None)
        tgt_parts = exchanged(sent, "x")
        given, first = (tgt_parts,), False

    def src_sums(picks, t_pot):
        return weighted_sums(True, picks, table, place, s_pot, t_pot, a, all_targets)

    def tgt_sums(picks, mine):
        return weighted_sums(False, picks, table, place, mine, s_pot, at, all_sources)

    tgt_far = tgt_sums(FAR, sent)
    tgt_far = far_sent(tgt_far, "x")
    t_pot, s_own, t_own, shares = final_potentials(place, s_pot, tgt_parts)
    src_far = src_sums(FAR, t_pot)
    src_far, t_pot = lax.optimization_barrier((src_far, t_pot))
    src_far = far_sent(src_far, "y")
    tgt_plain = tgt_sums(PLAIN, t_pot)
    tgt_plain, t_pot = lax.optimization_barrier((tgt_plain, t_pot))
    tgt_plain = plain_sent(tgt_plain, "x")
    src_near = src_sums(PLAIN + JOINT, t_pot)
    src_near, t_pot = lax.optimization_barrier((src_near, t_pot))
    src_plain = plain_sent(src_near[0:2], "y")
    tgt_near = tgt_sums(JOINT + HOME, t_pot)
    tgt_near, tgt_far = lax.optimization_barrier((tgt_near, tgt_far))
    tgt_joint = joint_sent(tgt_near[0:2], tgt_far, "x", shares)
    src_joint = joint_sent(src_near[2:4], src_far, "y")
    late = t_pot
    src_home = src_sums(HOME, late)
    tgt_home = tgt_near[2:4]
    tgt_mean = mean_of(*([tgt_home[k], tgt_plain[k], tgt_joint[k]] for k in range(2)))
    src_mean = mean_of(*([src_home[k], src_plain[k], src_joint[k]] for k in range(2)))
    return src_mean, tgt_mean, s_own.reshape(-1), t_own.reshape(-1)


def solution(mesh):
    wide, narrow = (mesh.shape[axis] for axis in ("wide", "narrow"))
    devices = mesh.devices.reshape(wide, SIDE, narrow // SIDE)
    grid = Mesh(devices, ("wide", "y", "x"))
    everyone = ("wide", "y", "x")
    in_specs = (
        P(everyone, None),
        P(everyone, None),
        P(everyone, None),
        P(everyone),
        P(everyone, None),
        P(NARROW, "wide"),
        P("wide"),
        P(NARROW),
    )
    out_specs = (P(everyone, None), P(everyone, None), P(everyone), P(everyone))
    return jax.shard_map(body, mesh=grid, in_specs=in_specs, out_specs=out_specs, check_vma=False)
```

```python
import functools

import jax
import jax.numpy as jnp
from jax import lax
from jax.experimental import pallas as pl
from jax.experimental.pallas import tpu as pltpu
from jax.sharding import Mesh
from jax.sharding import PartitionSpec as P

BLK = 128
LIST = 4
ITC = 6
STEPS = 3
CAP = 3
HEAT = 0.02
SIDE = 4
OWN = 8
GROUP = SIDE * OWN
UNROLL = 4
SLOTS = SIDE * SIDE * CAP + UNROLL
HALF = OWN // 2
HALF_ROWS = HALF * BLK + 16
FAR, PLAIN, JOINT, HOME = (4, 5), (6, 3), (2, 7), (0, 1)
NEG = -1e30
AT_SRC, AT_TGT, AT_START, AT_COUNT, AT_LIST, AT_LIVE, TABLE = 0, 64, 128, 168, 200, 712, 768
LINES = 3 * OWN + 1

F32 = jnp.float32
BF16 = jnp.bfloat16


def spec(n):
    return [pl.BlockSpec(memory_space=pltpu.VMEM)] * n


def smem(n):
    return [pl.BlockSpec(memory_space=pltpu.SMEM)] * n


def columns_of(rows):
    count = rows.shape[0]
    if count < BLK:
        rows = jnp.concatenate([rows, jnp.zeros((BLK - count, BLK), F32)], axis=0)
    return rows.T


def spread(col_ref, columns, count):
    for k in range(count):
        col_ref[k] = jnp.broadcast_to(columns[:, k : k + 1], (BLK, BLK))


def joined(parts_ref, rows=None):
    parts = [parts_ref[k, 0:rows, :] for k in range(parts_ref.shape[0])]
    top = tree(parts, jnp.maximum)
    return top + jnp.log(tree([jnp.exp(part - top) for part in parts], jnp.add))


def tree(parts, op):
    while len(parts) > 1:
        parts = [op(a, b) for a, b in zip(parts[::2], parts[1::2])] + (
            [parts[-1]] if len(parts) % 2 else []
        )
    return parts[0]


def coarse_cost_kernel(scale, place_ref, x_ref, *refs):
    pieces, (by_col_ref, by_row_ref, y_ref, ysq_ref) = refs[:SIDE], refs[SIDE:]
    z, core = place_ref[2], place_ref[3]
    depth, cols = pieces[0].shape[1], y_ref.shape[1] // BLK
    for away in range(SIDE):
        home = lax.rem(z + SIDE - away, SIDE) * 2
        for twin in range(2):
            at = (home + lax.rem(core + twin, 2)) * depth
            y_ref[pl.ds(pl.multiple_of(at, depth), depth), :] = pieces[away][twin]
    for k in range(cols):
        wide_y = y_ref[:, k * BLK : (k + 1) * BLK].astype(F32)
        ysq_ref[k : k + 1, :] = jnp.sum(wide_y * wide_y, axis=0, keepdims=True)
    tall = 2 * BLK

    def one(j, carry):
        x = x_ref[pl.ds(pl.multiple_of(j * tall, tall), tall), :]
        wide_x = x.astype(F32)
        x_sq = jnp.sum(wide_x * wide_x, axis=1, keepdims=True)
        for k in range(cols):
            y = y_ref[:, k * BLK : (k + 1) * BLK]
            cross = jnp.dot(x, y, preferred_element_type=F32)
            cost = (x_sq + ysq_ref[k : k + 1, :] - 2.0 * cross) * scale
            by_col_ref[k, pl.ds(pl.multiple_of(j * tall, tall), tall), :] = cost
            for h in range(2):
                by_row_ref[2 * j + h, k * BLK : (k + 1) * BLK, :] = cost[
                    h * BLK : (h + 1) * BLK, :
                ].T
        return carry

    lax.fori_loop(0, x_ref.shape[0] // tall, one, 0)


def coarse_costs(place, x, pieces, scale):
    rows, cols = x.shape[0] // BLK, pieces[0].shape[2] // BLK
    return pl.pallas_call(
        functools.partial(coarse_cost_kernel, scale),
        out_shape=(
            jax.ShapeDtypeStruct((cols, rows * BLK, BLK), F32),
            jax.ShapeDtypeStruct((rows, cols * BLK, BLK), F32),
        ),
        in_specs=smem(1) + spec(1 + SIDE),
        out_specs=tuple(spec(2)),
        scratch_shapes=[
            pltpu.VMEM((x.shape[1], cols * BLK), BF16),
            pltpu.VMEM((8, BLK), F32),
        ],
        compiler_params=pltpu.CompilerParams(vmem_limit_bytes=20 << 20),
        name="coarse_costs",
    )(place, x, *pieces)


def coarse_half_kernel(first, recv_ref, mass_ref, cost_ref, out_ref, col_ref, res_ref):
    given = mass_ref.shape[0]
    chunks = cost_ref.shape[0]
    if first:
        potential = jnp.zeros((given, BLK), F32)
    else:
        potential = jnp.log(mass_ref[...]) - joined(recv_ref, given)
    spread(col_ref, columns_of(potential), given)

    def chunk(c, carry):
        def piece(k):
            cost = cost_ref[c, k * BLK : (k + 1) * BLK, :]
            return (col_ref[k] - cost).reshape(BLK // 8, 8, BLK)

        top = tree([jnp.max(piece(k), axis=0) for k in range(given)], jnp.maximum)
        total = tree(
            [jnp.sum(jnp.exp(piece(k) - top[None]), axis=0) for k in range(given)], jnp.add
        )
        best = jnp.max(top, axis=0, keepdims=True)
        total = jnp.sum(total * jnp.exp(top - best), axis=0, keepdims=True)
        res_ref[pl.ds(c, 1), :] = best + jnp.log(total)
        return carry

    lax.fori_loop(0, chunks, chunk, 0)
    result = res_ref[0:chunks, :]
    for k in range(out_ref.shape[0]):
        out_ref[k, 0:chunks, :] = result
        if first:
            out_ref[k, chunks:, :] = recv_ref[...]


def coarse_half(first, recv, mass, cost, copies):
    given, chunks = mass.shape[0], cost.shape[0]
    lines = chunks + (recv.shape[0] if first else 0)
    return pl.pallas_call(
        functools.partial(coarse_half_kernel, first),
        out_shape=jax.ShapeDtypeStruct((copies, lines, BLK), F32),
        in_specs=spec(3),
        out_specs=spec(1)[0],
        scratch_shapes=[pltpu.VMEM((given, BLK, BLK), F32), pltpu.VMEM((8, BLK), F32)],
        compiler_params=pltpu.CompilerParams(vmem_limit_bytes=12 << 20),
        name="coarse_half",
    )(recv, mass, cost)


def coarse_end_kernel(recv_ref, mass_ref, out_ref):
    potential = jnp.log(mass_ref[...]) - joined(recv_ref)
    for k in range(out_ref.shape[0]):
        out_ref[k] = potential


def coarse_end(recv, mass, copies):
    return pl.pallas_call(
        coarse_end_kernel,
        out_shape=jax.ShapeDtypeStruct((copies, *mass.shape), F32),
        in_specs=spec(2),
        out_specs=spec(1)[0],
        name="coarse_end",
    )(recv, mass)


def plan_kernel(lists_ref, place_ref, table_ref):
    y = place_ref[0]

    def clear(k, carry):
        for j in range(8):
            table_ref[k * 8 + j] = 0
        return carry

    lax.fori_loop(0, TABLE // 8, clear, 0)

    def scan(q, live):
        block = lists_ref[q]
        device = lax.rem(lax.div(block, OWN), SIDE * SIDE)
        here = (lax.div(device, SIDE) == y).astype(jnp.int32)
        s = lax.div(q, LIST)
        t = lax.rem(device, SIDE) * OWN + lax.rem(block, OWN)
        table_ref[AT_SRC + live] = s
        table_ref[AT_TGT + live] = t
        seen = table_ref[AT_COUNT + t]
        table_ref[AT_LIST + t * 16 + seen] = live
        table_ref[AT_COUNT + t] = seen + here
        live = live + here
        table_ref[AT_START + s + 1] = live
        return live

    live = lax.fori_loop(0, SIDE * OWN * LIST, scan, 0)
    for k in range(UNROLL + 1):
        table_ref[AT_SRC + live + k] = GROUP
        table_ref[AT_TGT + live + k] = GROUP
    table_ref[AT_LIVE] = live


def entry_table(lists, place):
    return pl.pallas_call(
        plan_kernel,
        out_shape=jax.ShapeDtypeStruct((TABLE,), jnp.int32),
        in_specs=smem(2),
        out_specs=smem(1)[0],
        name="entry_table",
    )(lists, place)


def fine_cost_kernel(scale, table_ref, x_ref, y_ref, xsq_ref, ysq_ref, a_ref, at_ref, col_ref):
    spread(col_ref, columns_of(xsq_ref[...]), GROUP)

    def some(r, carry):
        for k in range(UNROLL):
            e = r * UNROLL + k
            s = jnp.minimum(table_ref[AT_SRC + e], GROUP - 1)
            t = jnp.minimum(table_ref[AT_TGT + e], GROUP - 1)
            cross = lax.dot_general(
                x_ref[s], y_ref[t], (((1,), (1,)), ((), ())), preferred_element_type=F32
            )
            cost = (col_ref[s] + ysq_ref[pl.ds(t, 1), :] - 2.0 * cross) * scale
            a_ref[e] = cost
            at_ref[e] = cost.T
        return carry

    lax.fori_loop(0, lax.div(table_ref[AT_LIVE] + (UNROLL - 1), UNROLL), some, 0)


def fine_costs(table, x, y, xsq, ysq, scale):
    shape = jax.ShapeDtypeStruct((SLOTS, BLK, BLK), F32)
    return pl.pallas_call(
        functools.partial(fine_cost_kernel, scale),
        out_shape=(shape, shape),
        in_specs=smem(1) + spec(4),
        out_specs=tuple(spec(2)),
        scratch_shapes=[pltpu.VMEM((GROUP, BLK, BLK), F32)],
        compiler_params=pltpu.CompilerParams(vmem_limit_bytes=24 << 20),
        name="fine_costs",
    )(table, x, y, xsq, ysq)


def looked_up(coarse_ref, ids_ref, pot_ref):
    rows = coarse_ref.shape[0]
    by_lane = columns_of(coarse_ref[...])[:, :rows]
    high = by_lane.astype(BF16)
    rest = by_lane - high.astype(F32)
    middle = rest.astype(BF16)
    low = (rest - middle.astype(F32)).astype(BF16)
    parts = jnp.concatenate([high, middle, low, jnp.zeros_like(low)], axis=1)
    depth = 4 * rows
    row_at = lax.rem(lax.broadcasted_iota(jnp.int32, (depth, BLK), 0), rows)
    lane_at = lax.broadcasted_iota(jnp.int32, (BLK, BLK), 0)

    def some(r, carry):
        for k in range(UNROLL):
            ids = ids_ref[pl.ds(r * UNROLL + k, 1), :]
            pick = jnp.where(row_at == (ids >> 7), 1.0, 0.0).astype(BF16)
            found = jnp.dot(parts, pick, preferred_element_type=F32)
            pot_ref[pl.ds(r * UNROLL + k, 1), :] = jnp.sum(
                jnp.where(lane_at == (ids & (BLK - 1)), found, 0.0), axis=0, keepdims=True
            )
        return carry

    lax.fori_loop(0, GROUP // UNROLL, some, 0)


def fine_half_kernel(first, last, given_at, into_at, *refs):
    *refs, col_ref, top_ref, sum_ref = refs
    if last:
        *refs, pot_ref = refs
    if first:
        table_ref, coarse_ref, ids_ref, mat_ref, out_ref = refs
        looked_up(coarse_ref, ids_ref, top_ref)
        potential = top_ref[0:GROUP, :]
    else:
        table_ref, recv_ref, mat_ref, out_ref = refs
        potential = -joined(recv_ref)
    if last:
        pot_ref[...] = potential
    spread(col_ref, columns_of(potential), GROUP)
    top_ref[...] = jnp.full(top_ref.shape, NEG, F32)
    sum_ref[...] = jnp.zeros(sum_ref.shape, F32)

    def some(r, carry):
        found = []
        for k in range(UNROLL):
            e = r * UNROLL + k
            given = jnp.minimum(table_ref[given_at + e], GROUP - 1)
            rating = (col_ref[given] - mat_ref[e]).reshape(BLK // 8, 8, BLK)
            top = jnp.max(rating, axis=0)
            total = jnp.sum(jnp.exp(rating - top[None]), axis=0)
            best = jnp.max(top, axis=0, keepdims=True)
            found.append((best, jnp.sum(total * jnp.exp(top - best), axis=0, keepdims=True)))
        for k in range(UNROLL):
            into = table_ref[into_at + r * UNROLL + k]
            row = pl.ds(into, 1)
            best, total = found[k]
            before = top_ref[row, :]
            now = jnp.maximum(before, best)
            sum_ref[row, :] = sum_ref[row, :] * jnp.exp(before - now) + total * jnp.exp(best - now)
            top_ref[row, :] = now
        return carry

    lax.fori_loop(0, lax.div(table_ref[AT_LIVE] + (UNROLL - 1), UNROLL), some, 0)
    result = top_ref[0:GROUP, :] + jnp.log(sum_ref[0:GROUP, :])
    for k in range(SIDE):
        out_ref[k] = result


def fine_half(first, last, given_at, into_at, table, given, mat):
    shapes = (
        jax.ShapeDtypeStruct((SIDE, GROUP, BLK), F32),
        jax.ShapeDtypeStruct((GROUP, BLK), F32),
    )
    return pl.pallas_call(
        functools.partial(fine_half_kernel, first, last, given_at, into_at),
        out_shape=shapes if last else shapes[0],
        in_specs=smem(1) + spec(len(given) + 1),
        out_specs=tuple(spec(2)) if last else spec(1)[0],
        scratch_shapes=[
            pltpu.VMEM((GROUP, BLK, BLK), F32),
            pltpu.VMEM((GROUP + 8, BLK), F32),
            pltpu.VMEM((GROUP + 8, BLK), F32),
        ],
        compiler_params=pltpu.CompilerParams(vmem_limit_bytes=16 << 20),
        name="fine_half",
    )(table, *given, mat)


def own_kernel(place_ref, s_ref, trecv_ref, t_ref, sown_ref, town_ref, share_ref):
    y, x = place_ref[0], place_ref[1]
    t_ref[...] = -joined(trecv_ref)

    def owned(device):
        return pl.ds(pl.multiple_of(device * OWN, OWN), OWN)

    sown_ref[...] = HEAT * s_ref[owned(y), :]
    town_ref[...] = HEAT * t_ref[owned(x), :]
    after, before = lax.rem(x + 1, SIDE), lax.rem(x + SIDE - 1, SIDE)
    for k, (sender, owner) in enumerate(((before, after), (after, before))):
        share = jnp.exp(trecv_ref[sender, owned(owner), :] + t_ref[owned(owner), :])
        share_ref[k, 0:HALF, :] = share[k * HALF : (k + 1) * HALF, :]
        share_ref[k, HALF:, :] = jnp.zeros((OWN - HALF, BLK), F32)


def final_potentials(place, s_pot, trecv):
    some = jax.ShapeDtypeStruct((GROUP, BLK), F32)
    own = jax.ShapeDtypeStruct((OWN, BLK), F32)
    return pl.pallas_call(
        own_kernel,
        out_shape=(some, own, own, jax.ShapeDtypeStruct((2, OWN, BLK), F32)),
        in_specs=smem(1) + spec(2),
        out_specs=tuple(spec(4)),
        compiler_params=pltpu.CompilerParams(vmem_limit_bytes=4 << 20),
        name="final_potentials",
    )(place, s_pot, trecv)


def masses_put(buf, mass):
    width = buf.shape[1]
    high = mass.astype(BF16).astype(F32)
    both = jnp.concatenate([high, mass - high, jnp.zeros((8, width - 2 * BLK), F32)], axis=1)
    buf[HALF * BLK :, :] = jnp.concatenate([both, jnp.zeros_like(both)], axis=0).astype(BF16)


def masses_of(tail):
    return tail[:, 0:BLK].astype(F32) + tail[:, BLK : 2 * BLK].astype(F32)


def sums_kernel(by_src, table_ref, place_ref, picks_ref, mine_ref, other_ref, mat_ref, rows_ref, *refs):
    *out_refs, acc_ref, mass_ref = refs
    q = pl.program_id(0)
    away, half = lax.div(picks_ref[q], 2), lax.rem(picks_ref[q], 2)
    base = lax.rem(place_ref[0 if by_src else 1] + away, SIDE) * OWN + half * HALF
    ones = jnp.ones((8, BLK), BF16)
    partner = AT_TGT if by_src else AT_SRC

    def term(block, k, column, live):
        if by_src:
            e = table_ref[AT_START + block] + k
        else:
            e = table_ref[AT_LIST + block * 16 + k]
        peer = jnp.minimum(table_ref[partner + e], GROUP - 1)
        plan = jnp.exp(column + other_ref[pl.ds(peer, 1), :] - mat_ref[e])
        if live is not None:
            plan = jnp.where(live, plan, 0.0)
        plan = plan.astype(BF16)
        total = jnp.dot(plan, rows_ref[peer], preferred_element_type=F32)
        mass = lax.dot_general(ones, plan, (((1,), (1,)), ((), ())), preferred_element_type=F32)
        return total, mass[0:1, :]

    def column_of(block):
        if len(mine_ref.shape) == 3:
            line = -mine_ref[0, pl.ds(block, 1), :]
        else:
            line = mine_ref[pl.ds(block, 1), :]
        return jnp.broadcast_to(line, (BLK, BLK)).T

    counts = []
    for b in range(HALF):
        block = base + b
        if by_src:
            count = table_ref[AT_START + block + 1] - table_ref[AT_START + block]
        else:
            count = table_ref[AT_COUNT + block]
        total, mass = term(block, 0, column_of(block), count > 0)
        acc_ref[b] = total
        mass_ref[b : b + 1, :] = mass
        counts.append(count)
    for b in range(HALF):

        def more(k, carry, b=b):
            total, mass = term(base + b, k, column_of(base + b), None)
            acc_ref[b] += total
            mass_ref[b : b + 1, :] += mass
            return carry

        lax.fori_loop(1, counts[b], more, 0)
    for k, out_ref in enumerate(out_refs):

        @pl.when(q == k)
        def _(out_ref=out_ref):
            for b in range(HALF):
                out_ref[b * BLK : (b + 1) * BLK, :] = acc_ref[b].astype(BF16)
            masses_put(out_ref, mass_ref[...])


def weighted_sums(by_src, picks, table, place, mine, other, mat, rows):
    width = rows.shape[2]
    return pl.pallas_call(
        functools.partial(sums_kernel, by_src),
        out_shape=(jax.ShapeDtypeStruct((HALF_ROWS, width), BF16),) * len(picks),
        grid=(len(picks),),
        in_specs=smem(3) + spec(4),
        out_specs=tuple(spec(len(picks))),
        scratch_shapes=[pltpu.VMEM((HALF, BLK, width), F32), pltpu.VMEM((8, BLK), F32)],
        compiler_params=pltpu.CompilerParams(vmem_limit_bytes=16 << 20),
        name="weighted_sums",
    )(table, place, jnp.array(picks, jnp.int32), mine, other, mat, rows)


def add_kernel(which, a_ref, b_ref, *refs):
    out_ref = refs[-1]
    tail = slice(HALF * BLK, HALF_ROWS)
    mass = masses_of(a_ref[tail, :])[0:OWN, :]
    if which is not None:
        mass = mass * refs[0][which]
    for b in range(HALF):
        rows = slice(b * BLK, (b + 1) * BLK)
        total = a_ref[rows, :].astype(F32)
        if which is not None:
            total = total * jnp.broadcast_to(refs[0][which, b : b + 1, :], (BLK, BLK)).T[:, 0:1]
        out_ref[rows, :] = (total + b_ref[rows, :].astype(F32)).astype(BF16)
    masses_put(out_ref, mass + masses_of(b_ref[tail, :])[0:OWN, :])


def added(a, b, which, shares):
    given = () if shares is None else (shares,)
    return pl.pallas_call(
        functools.partial(add_kernel, None if shares is None else which),
        out_shape=jax.ShapeDtypeStruct(a.shape, BF16),
        in_specs=spec(2 + len(given)),
        out_specs=spec(1)[0],
        compiler_params=pltpu.CompilerParams(vmem_limit_bytes=8 << 20),
        name="added",
    )(a, b, *given)


def mean_kernel(*refs):
    ins, out_ref = refs[:-1], refs[-1]
    step = pl.program_id(0)

    def give(rows, tails, b):
        mass = masses_of(tails[0])
        total = rows[0][...].astype(F32)
        for row, tail in zip(rows[1:], tails[1:]):
            mass = mass + masses_of(tail)
            total = total + row[...].astype(F32)
        for k in range(2):
            pick = lax.broadcasted_iota(jnp.int32, mass.shape, 0) == 2 * b + k
            line = jnp.sum(jnp.where(pick, mass, 0.0), axis=0, keepdims=True)
            share = jnp.broadcast_to(1.0 / line, (BLK, BLK)).T
            here = slice(k * BLK, (k + 1) * BLK)
            out_ref[here, :] = (total[here, :] * share[:, 0:1]).astype(BF16)

    @pl.when(step < HALF // 2)
    def _():
        give(ins[0:3], ins[6:9], step)

    @pl.when(step >= HALF // 2)
    def _():
        give(ins[3:6], ins[9:12], step - HALF // 2)


def mean_of(low, high):
    width = low[0].shape[1]
    loads, rows, tails = [*low, *high], [], []
    for at in (lambda b: jnp.minimum(b, HALF // 2 - 1), lambda b: jnp.maximum(b - HALF // 2, 0)):
        rows += [pl.BlockSpec((2 * BLK, width), lambda b, at=at: (at(b), 0))] * 3
        tails += [pl.BlockSpec((16, width), lambda b: (HALF * BLK // 16, 0))] * 3
    return pl.pallas_call(
        mean_kernel,
        out_shape=jax.ShapeDtypeStruct((OWN * BLK, width), BF16),
        grid=(OWN // 2,),
        in_specs=rows + tails,
        out_specs=pl.BlockSpec((2 * BLK, width), lambda b: (b, 0)),
        compiler_params=pltpu.CompilerParams(vmem_limit_bytes=16 << 20),
        name="mean_of",
    )(*loads, *loads)


NARROW = ("y", "x")


def exchanged(copies, axis):
    return lax.all_to_all(copies, axis, split_axis=0, concat_axis=0, tiled=True)


def copied(value, axis):
    count = lax.axis_size(axis) if isinstance(axis, str) else SIDE * SIDE
    return exchanged(jnp.broadcast_to(value, (count, *value.shape)), axis)


def shifted(value, axis, away):
    return lax.ppermute(value, axis, [(k, (k + away) % SIDE) for k in range(SIDE)])


def far_sent(far, axis):
    return shifted(far[0], axis, 1), shifted(far[1], axis, -1)


def plain_sent(plain, axis):
    return shifted(plain[0], axis, -1), shifted(plain[1], axis, 1)


def joint_sent(joint, far, axis, shares=None):
    low = shifted(added(far[0], joint[0], 0, shares), axis, 1)
    return low, shifted(added(far[1], joint[1], 1, shares), axis, -1)


def beside_core(value):
    return lax.ppermute(value, "wide", [(k, k ^ 1) for k in range(2 * SIDE)])


def along_z(value, away):
    ring = [(k, (k // 2 + away) % SIDE * 2 + k % 2) for k in range(2 * SIDE)]
    return lax.ppermute(value, "wide", ring)


def unpacked(facts, place):
    facts = facts.reshape(SIDE, SIDE, LINES, BLK)
    of_column = lax.dynamic_index_in_dim(facts, place[1], axis=1, keepdims=False)
    of_row = lax.dynamic_index_in_dim(facts, place[0], axis=0, keepdims=False)
    lists = of_column[:, 0, : OWN * LIST].astype(jnp.int32).reshape(-1)
    ids = of_row[:, 1 : 1 + OWN].astype(jnp.int32).reshape(GROUP, BLK)
    src_sq = of_column[:, 1 + OWN : 1 + 2 * OWN].reshape(GROUP, BLK)
    tgt_sq = of_row[:, 1 + 2 * OWN :].reshape(GROUP, BLK)
    return entry_table(lists, place), ids, src_sq, tgt_sq


def square_norms(rows):
    return jnp.sum(jnp.square(rows.astype(F32)), axis=-1)


def body(
    sources,
    targets,
    target_lists,
    target_clusters,
    centroids_src,
    centroids_tgt,
    sender_mean_measure,
    recipient_mean_measure,
):
    width = sources.shape[1]
    wide = lax.axis_size("wide")
    narrow = SIDE * SIDE
    scale = 1.0 / (width * HEAT)
    y, x = lax.axis_index("y"), lax.axis_index("x")
    w = lax.axis_index("wide")
    place = jnp.stack([y, x, w // 2, w % 2]).astype(jnp.int32)

    rows = copied(centroids_src, NARROW).reshape(-1, width)
    cols = centroids_tgt.T
    cols = jnp.stack([cols, beside_core(cols)])
    cols = [cols] + [along_z(cols, away) for away in range(1, SIDE)]

    facts = jnp.concatenate(
        [
            jnp.pad(target_lists.reshape(1, -1).astype(F32), ((0, 0), (0, BLK - OWN * LIST))),
            target_clusters.reshape(OWN, BLK).astype(F32),
            square_norms(sources).reshape(OWN, BLK),
            square_norms(targets).reshape(OWN, BLK),
        ],
        axis=0,
    )
    rows, cols, facts, sources, targets = lax.optimization_barrier(
        (rows, cols, facts, sources, targets)
    )
    all_targets = lax.all_gather(targets, "x", axis=0).reshape(GROUP, BLK, width)
    all_sources = lax.all_gather(sources, "y", axis=0).reshape(GROUP, BLK, width)

    by_col, by_row = coarse_costs(place, rows, cols, scale)
    row_mass = sender_mean_measure.reshape(-1, BLK)
    col_mass = recipient_mean_measure.reshape(-1, BLK)
    recv = facts
    for turn in range(ITC):
        sent = coarse_half(turn == 0, recv, col_mass, by_row, narrow)
        got = exchanged(sent, NARROW)
        sent = coarse_half(False, got, row_mass, by_col, wide)
        if turn == 0:
            sent, got = lax.optimization_barrier((sent, got))
            table, ids, src_sq, tgt_sq = unpacked(got[:, OWN:], place)
            recv = exchanged(sent, "wide")
            recv, table, ids, src_sq, tgt_sq = lax.optimization_barrier((recv, table, ids, src_sq, tgt_sq))
        else:
            recv = exchanged(sent, "wide")
    sent = coarse_end(recv, col_mass, narrow)
    sent, table = lax.optimization_barrier((sent, table))
    a, at = fine_costs(table, all_sources, all_targets, src_sq, tgt_sq, scale)
    coarse = exchanged(sent, NARROW).reshape(-1, BLK)

    given, first = (coarse, ids), True
    for step in range(STEPS):
        last = step == STEPS - 1
        sent = fine_half(first, False, AT_TGT, AT_SRC, table, given, at)
        src_parts = exchanged(sent, "y")
        sent = fine_half(False, last, AT_SRC, AT_TGT, table, (src_parts,), a)
        sent, s_pot = sent if last else (sent, None)
        tgt_parts = exchanged(sent, "x")
        given, first = (tgt_parts,), False

    def src_sums(picks, t_pot):
        return weighted_sums(True, picks, table, place, s_pot, t_pot, a, all_targets)

    def tgt_sums(picks, mine):
        return weighted_sums(False, picks, table, place, mine, s_pot, at, all_sources)

    tgt_far = tgt_sums(FAR, sent)
    tgt_far = far_sent(tgt_far, "x")
    t_pot, s_own, t_own, shares = final_potentials(place, s_pot, tgt_parts)
    src_far = src_sums(FAR, t_pot)
    src_far, t_pot = lax.optimization_barrier((src_far, t_pot))
    src_far = far_sent(src_far, "y")
    tgt_plain = tgt_sums(PLAIN, t_pot)
    tgt_plain, t_pot = lax.optimization_barrier((tgt_plain, t_pot))
    tgt_plain = plain_sent(tgt_plain, "x")
    src_near = src_sums(PLAIN + JOINT, t_pot)
    src_near, t_pot = lax.optimization_barrier((src_near, t_pot))
    src_plain = plain_sent(src_near[0:2], "y")
    tgt_near = tgt_sums(JOINT + HOME, t_pot)
    tgt_near, tgt_far = lax.optimization_barrier((tgt_near, tgt_far))
    tgt_joint = joint_sent(tgt_near[0:2], tgt_far, "x", shares)
    src_joint = joint_sent(src_near[2:4], src_far, "y")
    late = t_pot
    src_home = src_sums(HOME, late)
    tgt_home = tgt_near[2:4]
    tgt_mean = mean_of(*([tgt_home[k], tgt_plain[k], tgt_joint[k]] for k in range(2)))
    src_mean = mean_of(*([src_home[k], src_plain[k], src_joint[k]] for k in range(2)))
    return src_mean, tgt_mean, s_own.reshape(-1), t_own.reshape(-1)


def solution(mesh):
    wide, narrow = (mesh.shape[axis] for axis in ("wide", "narrow"))
    devices = mesh.devices.reshape(wide, SIDE, narrow // SIDE)
    grid = Mesh(devices, ("wide", "y", "x"))
    everyone = ("wide", "y", "x")
    in_specs = (
        P(everyone, None),
        P(everyone, None),
        P(everyone, None),
        P(everyone),
        P(everyone, None),
        P(NARROW, "wide"),
        P("wide"),
        P(NARROW),
    )
    out_specs = (P(everyone, None), P(everyone, None), P(everyone), P(everyone))
    return jax.shard_map(body, mesh=grid, in_specs=in_specs, out_specs=out_specs, check_vma=False)
```
